32 devices in a mesh: seq: 8 (over y, x, core), fsdp: 4 (over z).
Axes of the slice: x: 2, y: 2, z: 4, core: 2. Of those that a mesh axis runs over, the one named last changes fastest.
Arguments:
- tokens: bfloat16 [4, 1024, 2048], P('fsdp', 'seq'), may hold values from -6 to 6
- cotangent: bfloat16 [4, 1024, 2048], P('fsdp', 'seq'), may hold values from -6 to 6
- lengths: int32 [4, 6], P('fsdp'), may hold values from 1 to 854, 1024 in all within a row
- priority: int32 [4, 1024], P('fsdp', 'seq'), may hold values from 0 to 1023, each once within a row
- routes: int32 [4, 1024, 8], P('fsdp', 'seq'), may hold values from 0 to 15, all different within a row
- attn_norm: bfloat16 [2048], P('fsdp'), may hold values from 0.099609375 to 1.8984375
- q_proj: bfloat16 [2048, 2048], P('fsdp', 'seq'), may hold values from -0.125 to 0.125
- k_proj: bfloat16 [2048, 2048], P('fsdp', 'seq'), may hold values from -0.125 to 0.125
- v_proj: bfloat16 [2048, 2048], P('fsdp', 'seq'), may hold values from -0.125 to 0.125
- o_proj: bfloat16 [2048, 2048], P('seq', 'fsdp'), may hold values from -0.5 to 0.5
- q_norm: bfloat16 [2048], P('fsdp'), may hold values from 0.099609375 to 1.8984375
- k_norm: bfloat16 [2048], P('fsdp'), may hold values from 0.099609375 to 1.8984375
- ffn_norm: bfloat16 [2048], P('fsdp'), may hold values from 0.099609375 to 1.8984375
- router: bfloat16 [2048, 16], P('fsdp'), may hold values from -0.125 to 0.125
- gate_proj: bfloat16 [16, 2048, 1024], P('seq', 'fsdp'), may hold values from -0.125 to 0.125
- up_proj: bfloat16 [16, 2048, 1024], P('seq', 'fsdp'), may hold values from -0.125 to 0.125
- down_proj: bfloat16 [16, 1024, 2048], P('seq', 'fsdp'), may hold values from -1.5 to 1.5
Outputs:
- out_tokens: bfloat16 [4, 1024, 2048], P('fsdp', 'seq')
- tokens_grad: float32 [4, 1024, 2048], P('fsdp', 'seq')
- attn_norm_grad: float32 [2048], P(('seq', 'fsdp'))
- q_proj_grad: float32 [2048, 2048], P('fsdp', 'seq')
- k_proj_grad: float32 [2048, 2048], P('fsdp', 'seq')
- v_proj_grad: float32 [2048, 2048], P('fsdp', 'seq')
- o_proj_grad: float32 [2048, 2048], P('seq', 'fsdp')
- q_norm_grad: float32 [2048], P(('seq', 'fsdp'))
- k_norm_grad: float32 [2048], P(('seq', 'fsdp'))
- ffn_norm_grad: float32 [2048], P(('seq', 'fsdp'))
- router_grad: float32 [2048, 16], P(('seq', 'fsdp'))
- gate_proj_grad: float32 [16, 2048, 1024], P('seq', 'fsdp')
- up_proj_grad: float32 [16, 2048, 1024], P('seq', 'fsdp')
- down_proj_grad: float32 [16, 1024, 2048], P('seq', 'fsdp')
The draws below stay inside these ranges and needn't reach their ends.
Inputs may be any that keep to these rules, and one draw needn't show every extreme that they name: The lengths of a group sum to 1024; in each group the longest is 854. `priority`: each group's entries are a permutation. `routes`: each token names 8 different experts.
All inputs are finite; a program needn't handle non-finite values.
Results may differ from the reference program's by a relative error of at most 0.024.
Values may be sent and summed in bfloat16 or wider, within the bound.
No kernel may reach another device: no remote copies, remote signals or barrier semaphores. Data moves between devices by JAX's collectives and lax.ppermute only.
A program may use at most 256 MiB of HBM per device.

```python
import math
from functools import partial
import jax
import jax.numpy as jnp
import numpy as np
from jax import lax

D = 2048
HEADS = 16
HEAD_DIM = 128
FF = 1024
TOP = 8
TOK_DEV = 128
Q_BLOCK = 512
NDOC = 6
GROUPS = 4
GROUP_TOK = 1024
EXPERTS = 16
CAP = 64
DOC_MOST = 854
N_SEQ = 8


def block_levels(own_key, shape, shards, least, top_value):
    level, own = 1.0, jax.random.fold_in(own_key, 6)
    for axis_at, blocks in shards:
        steps = jnp.exp(jax.random.uniform(jax.random.fold_in(own, axis_at), (blocks,), jnp.float32, least / len(shards), top_value / len(shards)))
        level = level * jnp.repeat(steps, shape[axis_at] // blocks).reshape([-1 if axis == axis_at else 1 for axis in range(len(shape))])
    return level


def choose_distinct(key, rows, amount, top, lift):
    ranking = jax.random.permutation(jax.random.fold_in(key, 1), amount)
    favour = ranking
    for power in range(3):
        favour = favour * favour // amount
    favour = favour * lift // amount
    lots = jax.random.randint(jax.random.fold_in(key, 2), (rows, amount), 0, 4096) + favour
    fixed_rows = jax.random.permutation(jax.random.fold_in(key, 3), rows)[jnp.arange(amount) % rows]
    lots = jnp.where(jnp.arange(rows)[:, None] == fixed_rows[None, :], 1 << 14, lots)
    score = lots * amount + jnp.arange(amount)
    return lax.top_k(score.astype(jnp.int32), top)[1].astype(jnp.int32)


def split_up(count, total, reach, lean):
    weights = [(1 << 20) // math.isqrt(grade ** lean) + 1 for grade in range(2, count + 1)]
    surplus, given = total - reach - (count - 1), [1] * (count - 1)
    while surplus > 0:
        free = [i for i in range(count - 1) if given[i] < reach]
        pool, left = sum([weights[i] for i in free]), surplus
        for i in free:
            more = min(reach - given[i], max(1, left * weights[i] // pool), surplus)
            given[i] = given[i] + more
            surplus = surplus - more
    return np.array([reach] + given)


def uneven_parts(rng, number_of, total, limit, skew):
    if number_of == 2:
        one = jax.random.randint(rng, (), max(1, total - limit), min(limit, total - 1) + 1)
        return jnp.stack([one, total - one])
    sizes = jnp.asarray(split_up(number_of, total, limit, skew), jnp.int32)
    pairs = (number_of - 1) // 2
    donor, taker = sizes[1:1 + 2 * pairs:2], sizes[2:2 + 2 * pairs:2]
    slack = jnp.minimum(donor - 1, limit - taker)
    moved = jax.random.randint(jax.random.fold_in(rng, 1), (pairs,), 0, 1 << 20) % (slack + 1)
    sizes = sizes.at[1:1 + 2 * pairs:2].set(donor - moved).at[2:2 + 2 * pairs:2].set(taker + moved)
    return sizes[jax.random.permutation(jax.random.fold_in(rng, 2), number_of)]


def bell_draw(key, extent, spread, reach, pieces=(), held_as=jnp.bfloat16):
    gain = block_levels(key, extent, pieces, -0.22, 0.18) if pieces else 1.0
    array = jax.random.normal(key, extent, jnp.float32) * spread * gain
    return jnp.minimum(jnp.maximum(array, -reach), reach).astype(held_as)


def setup_inputs(seed: int = 0) -> dict:
    key_of = jax.random.split(jax.random.key(seed), 18)
    tokens = bell_draw(key_of[0], (GROUPS, GROUP_TOK, D), 1.0, 6.0, ((0, 4), (1, 8)))
    cotangent = bell_draw(key_of[1], (GROUPS, GROUP_TOK, D), 1.0, 6.0, ((0, 4), (1, 8)))
    lengths = jax.vmap(lambda own: uneven_parts(own, NDOC, GROUP_TOK, DOC_MOST, 2))(jax.random.split(key_of[2], GROUPS)).reshape((GROUPS, NDOC)).astype(jnp.int32)
    priority = jax.vmap(lambda own: jax.random.permutation(own, GROUP_TOK))(jax.random.split(key_of[3], GROUPS)).reshape((GROUPS, GROUP_TOK)).astype(jnp.int32)
    routes = choose_distinct(key_of[4], GROUPS * GROUP_TOK, EXPERTS, TOP, 4096).reshape((GROUPS, GROUP_TOK, TOP))
    attn_norm = jnp.clip(1.0 + 0.18 * jax.random.normal(key_of[5], (D,), jnp.float32), 0.099609375, 1.8984375).astype(jnp.bfloat16)
    q_proj = bell_draw(key_of[6], (D, D), D ** -0.5, 0.125, ((0, 4), (1, 8)))
    k_proj = bell_draw(key_of[7], (D, D), D ** -0.5, 0.125, ((0, 4), (1, 8)))
    v_proj = bell_draw(key_of[8], (D, D), D ** -0.5, 0.125, ((0, 4), (1, 8)))
    o_proj = bell_draw(key_of[9], (D, D), (D // 16) ** -0.5, 0.5, ((0, 8), (1, 4)))
    q_norm = jnp.clip(1.0 + 0.18 * jax.random.normal(key_of[10], (D,), jnp.float32), 0.099609375, 1.8984375).astype(jnp.bfloat16)
    k_norm = jnp.clip(1.0 + 0.18 * jax.random.normal(key_of[11], (D,), jnp.float32), 0.099609375, 1.8984375).astype(jnp.bfloat16)
    ffn_norm = jnp.clip(1.0 + 0.18 * jax.random.normal(key_of[12], (D,), jnp.float32), 0.099609375, 1.8984375).astype(jnp.bfloat16)
    router = bell_draw(key_of[13], (D, EXPERTS), D ** -0.5, 0.125, ((0, 4),))
    gate_proj = bell_draw(key_of[14], (EXPERTS, D, FF), D ** -0.5, 0.125, ((0, 8), (1, 4)))
    up_proj = bell_draw(key_of[15], (EXPERTS, D, FF), D ** -0.5, 0.125, ((0, 8), (1, 4)))
    down_proj = bell_draw(key_of[16], (EXPERTS, FF, D), (max(FF // 64, 1)) ** -0.5, 1.5, ((0, 8), (1, 4)))
    return {"tokens": tokens, "cotangent": cotangent, "lengths": lengths, "priority": priority, "routes": routes, "attn_norm": attn_norm, "q_proj": q_proj, "k_proj": k_proj, "v_proj": v_proj, "o_proj": o_proj, "q_norm": q_norm, "k_norm": k_norm, "ffn_norm": ffn_norm, "router": router, "gate_proj": gate_proj, "up_proj": up_proj, "down_proj": down_proj}


NORM_EPSILON = 1e-05
ROPE_THETA = 10000.0
MASKED = -1e+30
HIGHEST = lax.Precision.HIGHEST

@jax.custom_vjp
def low(v):
    return lax.optimization_barrier(v.astype(jnp.bfloat16)).astype(jnp.float32)

@jax.custom_vjp
def low_back(v):
    return v

def low_keep(v):
    return (low(v), None)

def low_pass(kept, grad):
    return (grad,)

def back_keep(v):
    return (v, None)

def back_low(kept, grad):
    return (low(grad),)
low.defvjp(low_keep, low_pass)
low_back.defvjp(back_keep, back_low)

def rms_norm(values, norm_gain):
    factor = lax.rsqrt(lax.optimization_barrier(jnp.mean(values * values, axis=-1, keepdims=True)) + NORM_EPSILON)
    return values * factor * norm_gain

def softmax_rows(logits):
    highest = lax.optimization_barrier(jnp.max(logits, axis=-1, keepdims=True))
    expon = jnp.exp(logits - highest)
    return expon / lax.optimization_barrier(jnp.sum(expon, axis=-1, keepdims=True))

def rotate(values, cosine_table, sine_table):
    middle = values.shape[-1] // 2
    leading = values[..., :middle]
    trailing = values[..., middle:]
    return jnp.concatenate([leading * cosine_table - trailing * sine_table, trailing * cosine_table + leading * sine_table], axis=-1)

def document_ids(lengths_row, positions):
    bounds = jnp.cumsum(lengths_row).astype(jnp.int32)
    doc_ids = lax.optimization_barrier(jnp.sum((positions[:, None] >= bounds[None, :]).astype(jnp.int32), axis=1)).astype(jnp.int32)
    return (doc_ids, (bounds - lengths_row).astype(jnp.int32))

def rope_tables(lengths_row, positions):
    doc_ids, starts = document_ids(lengths_row, positions)
    labels = jnp.arange(lengths_row.shape[0], dtype=jnp.int32)
    offsets = lax.optimization_barrier(jnp.sum((doc_ids[:, None] == labels[None, :]).astype(jnp.int32) * starts[None, :], axis=1)).astype(jnp.int32)
    places = (positions - offsets).astype(jnp.float32)
    middle = HEAD_DIM // 2
    frequency = 1.0 / ROPE_THETA ** (jnp.arange(middle, dtype=jnp.float32) * 2.0 / HEAD_DIM)
    angles = places[:, None] * frequency[None, :]
    return (doc_ids, jnp.cos(angles)[:, None, :], jnp.sin(angles)[:, None, :])

def route_tables(chosen_ids, priority_row, experts, capacity):
    count = chosen_ids.shape[0]
    labels = jnp.arange(experts, dtype=jnp.int32)
    chosen = lax.optimization_barrier(jnp.sum((chosen_ids[:, :, None] == labels[None, None, :]).astype(jnp.int32), axis=1)).astype(jnp.int32)
    earlier = (priority_row[None, :] < priority_row[:, None]).astype(jnp.int32)
    ranks = jnp.dot(earlier, chosen, preferred_element_type=jnp.int32).astype(jnp.int32)
    kept = chosen * (ranks < capacity).astype(jnp.int32)
    route_rank = jnp.take_along_axis(ranks, chosen_ids, axis=1)
    slot_of = jnp.where(route_rank < capacity, chosen_ids * capacity + route_rank, experts * capacity).astype(jnp.int32)
    places = jnp.arange(capacity, dtype=jnp.int32)
    matches = kept[:, :, None] * (ranks[:, :, None] == places[None, None, :]).astype(jnp.int32)
    filled = lax.optimization_barrier(jnp.sum(matches, axis=0)).astype(jnp.int32)
    token_index = jnp.arange(count, dtype=jnp.int32)
    slot_source = (lax.optimization_barrier(jnp.sum(matches * token_index[:, None, None], axis=0)) + (1 - filled) * count).astype(jnp.int32)
    return (slot_of, slot_source.reshape(experts * capacity))

def attend(queries, keys, values, doc_ids, positions):
    scaling = HEAD_DIM ** (-0.5)

    def one_block(begin_row):
        block_query = lax.dynamic_slice_in_dim(queries, begin_row, Q_BLOCK, 0)
        raw_scores = low_back(jnp.einsum('bhd,thd->hbt', block_query, keys, precision=HIGHEST))
        rows_here = begin_row + jnp.arange(Q_BLOCK, dtype=jnp.int32)
        row_docs = lax.dynamic_slice_in_dim(doc_ids, begin_row, Q_BLOCK, 0)
        allowed = (row_docs[:, None] == doc_ids[None, :]) & (positions[None, :] <= rows_here[:, None])
        logits = jnp.where(allowed[None], raw_scores * scaling, MASKED)
        weights_soft = softmax_rows(logits)
        return jnp.einsum('hbt,thd->bhd', low(weights_soft), values, precision=HIGHEST)
    begins = jnp.arange(GROUP_TOK // Q_BLOCK, dtype=jnp.int32) * Q_BLOCK
    blocks = lax.map(jax.checkpoint(one_block), begins)
    return blocks.reshape(GROUP_TOK, HEADS * HEAD_DIM)

def group_forward(inputs, lengths_row, combine_index, dispatch_index, chosen_ids, params):
    attn_gain, wquery, wkey, wvalue, wout, query_gain, key_gain, ffn_gain, router_w, gate_w, up_w, down_w = params
    total_rows = inputs.shape[0]
    model_width = inputs.shape[1]
    positions = jnp.arange(total_rows, dtype=jnp.int32)
    doc_ids, cosine_table, sine_table = rope_tables(lengths_row, positions)
    head_shape = (total_rows, HEADS, HEAD_DIM)
    attn_in = low(rms_norm(inputs, attn_gain))
    query_raw = low_back(jnp.dot(attn_in, wquery, precision=HIGHEST))
    key_raw = low_back(jnp.dot(attn_in, wkey, precision=HIGHEST))
    value_low = low_back(low(jnp.dot(attn_in, wvalue, precision=HIGHEST))).reshape(head_shape)
    query_rot = low_back(low(rotate(rms_norm(query_raw, query_gain).reshape(head_shape), cosine_table, sine_table)))
    key_rot = low_back(low(rotate(rms_norm(key_raw, key_gain).reshape(head_shape), cosine_table, sine_table)))
    attended = low_back(low(attend(query_rot, key_rot, value_low, doc_ids, positions)))
    residual = inputs + low_back(jnp.dot(attended, wout, precision=HIGHEST))
    ffn_in = low(rms_norm(residual, ffn_gain))
    router_logits = low_back(jnp.dot(ffn_in, router_w, precision=HIGHEST))
    router_probs = softmax_rows(router_logits)
    padded_in = jnp.concatenate([ffn_in, jnp.zeros((1, model_width), jnp.float32)], axis=0)
    arrived = low_back(padded_in[dispatch_index])
    gate_value = low_back(jnp.einsum('esd,edf->esf', arrived, gate_w, precision=HIGHEST))
    up_value = low_back(jnp.einsum('esd,edf->esf', arrived, up_w, precision=HIGHEST))
    hidden = low(gate_value * jax.nn.sigmoid(gate_value) * up_value)
    expert_out = low_back(low(jnp.einsum('esf,efd->esd', hidden, down_w, precision=HIGHEST)))
    flat_out = jnp.concatenate([expert_out.reshape(-1, model_width), jnp.zeros((1, model_width), jnp.float32)], axis=0)
    route_weight = jnp.take_along_axis(router_probs, chosen_ids, axis=1)
    picked = flat_out[combine_index]
    return residual + lax.optimization_barrier(jnp.sum(route_weight[:, :, None] * picked, axis=1))

def reference(tokens, cotangent, lengths, priority, routes, attn_norm, q_proj, k_proj, v_proj, o_proj, q_norm, k_norm, ffn_norm, router, gate_proj, up_proj, down_proj):
    block_count = GROUPS * N_SEQ
    block_routes = routes.reshape(block_count, TOK_DEV, TOP)
    block_order = priority.reshape(block_count, TOK_DEV)
    slot_of, slot_source = jax.vmap(partial(route_tables, experts=EXPERTS, capacity=CAP))(block_routes, block_order)
    block_ids = (jnp.arange(block_count, dtype=jnp.int32) % N_SEQ).astype(jnp.int32)
    dispatch = jnp.where(slot_source < TOK_DEV, block_ids[:, None] * TOK_DEV + slot_source, GROUP_TOK).astype(jnp.int32)
    dispatch = dispatch.reshape(GROUPS, N_SEQ, EXPERTS, CAP).transpose(0, 2, 1, 3).reshape(GROUPS, EXPERTS, N_SEQ * CAP)
    expert_of = slot_of // CAP
    place_of = slot_of % CAP
    combine = jnp.where(slot_of < EXPERTS * CAP, (expert_of * N_SEQ + block_ids[:, None, None]) * CAP + place_of, EXPERTS * N_SEQ * CAP).astype(jnp.int32)
    combine = combine.reshape(GROUPS, GROUP_TOK, TOP)
    params = tuple((weight.astype(jnp.float32) for weight in (attn_norm, q_proj, k_proj, v_proj, o_proj, q_norm, k_norm, ffn_norm, router, gate_proj, up_proj, down_proj)))

    def forward(inputs, weights):

        def one_group(carry, items):
            group_in, lengths_row, combine_index, dispatch_index, chosen_ids = items
            return (carry, jax.checkpoint(group_forward)(group_in, lengths_row, combine_index, dispatch_index, chosen_ids, weights))
        unused, results = lax.scan(one_group, jnp.int32(0), (inputs, lengths, combine, dispatch, routes))
        return results
    outputs, pull = jax.vjp(forward, tokens.astype(jnp.float32), params)
    grad_inputs, grads = pull(cotangent.astype(jnp.float32))
    return (outputs.astype(jnp.bfloat16), grad_inputs, grads[0], grads[1], grads[2], grads[3], grads[4], grads[5], grads[6], grads[7], grads[8], grads[9], grads[10], grads[11])
```

```python
import jax
import jax.numpy as jnp
from jax import lax
from jax.sharding import PartitionSpec as P

HEADS = 16
HEAD_DIM = 128
TOP = 8
NORM_EPSILON = 1e-05
ROPE_THETA = 10000.0
MASKED = -1e30
BF = jnp.bfloat16
F32 = jnp.float32


def mm(a, b, dims):
    return lax.dot_general(a, b, dims, preferred_element_type=F32)


NN = (((1,), (0,)), ((), ()))
NT = (((1,), (1,)), ((), ()))
TN = (((0,), (0,)), ((), ()))


def norm_factor(values):
    return lax.rsqrt(jnp.mean(values * values, axis=-1, keepdims=True) + NORM_EPSILON)


def norm_back(grad_out, norm_gain, normed, factor):
    grad_normed = grad_out * norm_gain
    inner = jnp.mean(grad_normed * normed, axis=-1, keepdims=True)
    return factor * (grad_normed - normed * inner)


def rotate(values, cosine, sine):
    middle = values.shape[-1] // 2
    a = values[..., :middle]
    b = values[..., middle:]
    return jnp.concatenate([a * cosine - b * sine, b * cosine + a * sine], axis=-1)


def documents(lengths_row, positions):
    bounds = jnp.cumsum(lengths_row)
    doc = jnp.sum((positions[:, None] >= bounds[None, :]).astype(jnp.int32), axis=1)
    labels = jnp.arange(lengths_row.shape[0], dtype=jnp.int32)
    starts = bounds - lengths_row
    offset = jnp.sum((doc[:, None] == labels[None, :]).astype(jnp.int32) * starts[None, :], axis=1)
    return doc, positions - offset


def body(
    tokens, cotangent, lengths, priority, routes, attn_norm, q_proj, k_proj, v_proj, o_proj,
    q_norm, k_norm, ffn_norm, router, gate_proj, up_proj, down_proj,
):
    n_seq = lax.axis_size("seq")
    n_fsdp = lax.axis_size("fsdp")
    s = lax.axis_index("seq")
    f = lax.axis_index("fsdp")
    columns = n_seq // 2
    tok = tokens.shape[1]
    width = tokens.shape[2]
    group = tok * n_seq
    heads = HEADS // n_seq
    head_width = heads * HEAD_DIM
    experts = router.shape[1]
    capacity = tok * TOP // experts
    shard = width // n_fsdp
    ff = gate_proj.shape[2]
    parts = n_fsdp // 2
    ff_part = ff // parts
    ff_piece = ff_part // n_fsdp
    column = s // 2
    core = s % 2

    def over_seq(x, bit):
        return lax.ppermute(x, "seq", [(i, i ^ bit) for i in range(n_seq)])

    def over_fsdp(x, bit):
        return lax.ppermute(x, "fsdp", [(i, i ^ bit) for i in range(n_fsdp)])

    def home_pairs(r, back):
        pairs = []
        for z in range(n_fsdp):
            for i in range(n_seq):
                place = (i % 2) * n_fsdp + (z ^ r)
                there = ((i // 2) * 2 + (place & 1)) * n_fsdp + (place >> 1)
                here = i * n_fsdp + z
                pairs.append((there, here) if back else (here, there))
        return pairs

    def gather_seq(x):
        own = [x] + [over_seq(x, 2 * d) for d in range(1, columns)]
        other = [over_seq(piece, 1) for piece in own]
        return jnp.concatenate(own + other, axis=0)

    def scatter_seq(near, far):
        far_sum = over_seq(far, 1)
        total = (near + far_sum.astype(F32)).reshape(columns, tok, width)
        low = total.astype(BF)
        result = total[0]
        for d in range(1, columns):
            result = result + over_seq(low[d], 2 * d).astype(F32)
        return result

    def sum_rows_seq(x):
        x = x + jnp.flip(over_seq(x, 1), axis=1)
        bit = 1
        while bit < columns:
            order = [d ^ bit for d in range(columns)]
            got = over_seq(x, 2 * bit)
            x = x + jnp.stack([got[:, :, d] for d in order], axis=2)
            bit *= 2
        return x

    def sum_all(x, axes):
        for name, count in axes:
            bit = 1
            while bit < count:
                x = x + (over_seq(x, bit) if name == "seq" else over_fsdp(x, bit))
                bit *= 2
        return x

    small = jnp.concatenate(
        [attn_norm, q_norm, k_norm, ffn_norm, router.T.reshape(-1)]
    ).reshape(1, -1)
    small_x = jnp.concatenate([small] + [over_fsdp(small, d) for d in range(1, n_fsdp)], axis=0)
    order = jnp.arange(n_fsdp, dtype=jnp.int32)
    pick = ((order[:, None] ^ f) == order[None, :]).astype(BF)
    small_n = mm(pick, small_x, NN)
    gains = small_n[:, : 4 * shard].reshape(n_fsdp, 4, shard).transpose(1, 0, 2).reshape(4, width)
    attn_gain, query_gain_all, key_gain_all, ffn_gain = gains[0], gains[1], gains[2], gains[3]
    router_t = (
        small_n[:, 4 * shard :].reshape(n_fsdp, experts, shard).transpose(1, 0, 2)
        .reshape(experts, width).astype(BF)
    )
    query_gain = lax.dynamic_slice_in_dim(query_gain_all, s * head_width, head_width, 0)
    key_gain = lax.dynamic_slice_in_dim(key_gain_all, s * head_width, head_width, 0)

    qkv_shard = jnp.concatenate([q_proj, k_proj, v_proj], axis=1)
    qkv = jnp.zeros((width, 3 * head_width), BF)
    qkv = lax.dynamic_update_slice(qkv, qkv_shard, (f * shard, 0))
    qkv_got = [over_fsdp(qkv_shard, d) for d in range(1, n_fsdp)]
    for d in range(1, n_fsdp):
        qkv = lax.dynamic_update_slice(qkv, qkv_got[d - 1], ((f ^ d) * shard, 0))
    out_w = jnp.zeros((head_width, width), BF)
    out_w = lax.dynamic_update_slice(out_w, o_proj, (0, f * shard))
    for d in range(1, n_fsdp):
        out_w = lax.dynamic_update_slice(out_w, over_fsdp(o_proj, d), (0, (f ^ d) * shard))

    labels = jnp.arange(experts, dtype=jnp.int32)
    chosen = jnp.sum((routes[0][:, :, None] == labels[None, None, :]).astype(F32), axis=1)
    earlier = (priority[0][None, :] < priority[0][:, None]).astype(BF)
    ranks = mm(earlier, chosen.astype(BF), NN)
    kept = (chosen > 0.5) & (ranks < capacity)
    table = jnp.where(kept, ranks, -1.0).astype(BF)
    table_x = jnp.stack([table] + [over_fsdp(table, d) for d in range(1, n_fsdp)])
    wanted = 4 * (column ^ jnp.arange(columns, dtype=jnp.int32)) + (4 * f) // n_fsdp
    select = (labels[:, None] == wanted[None, :]).astype(BF)
    slot_col = jnp.einsum("gte,ed->dgt", table_x, select, preferred_element_type=F32)
    slots = jnp.arange(capacity, dtype=jnp.int32).astype(F32)
    onehot = (slot_col[:, :, None, :] == slots[None, None, :, None]).astype(BF)

    def dispatch(everything):
        pieces = []
        for d in range(columns):
            piece = jnp.einsum(
                "grt,gtx->grx", onehot[d], everything, preferred_element_type=F32
            ).astype(BF)
            pieces.append(over_seq(piece, 2 * d) if d else piece)
        return pieces

    def both_cores(pieces):
        far = [over_seq(piece, 1) for piece in pieces]
        return jnp.concatenate(
            [piece.reshape(-1, piece.shape[-1]) for piece in pieces + far], axis=0
        )

    gate_pieces = (
        gate_proj.reshape(2, shard, n_fsdp, parts, ff_piece).transpose(0, 3, 1, 2, 4)
        .reshape(2 * parts, shard, ff_part)
    )
    up_pieces = (
        up_proj.reshape(2, shard, n_fsdp, parts, ff_piece).transpose(0, 3, 1, 2, 4)
        .reshape(2 * parts, shard, ff_part)
    )
    down_pieces = down_proj.reshape(2 * parts, ff_piece, width)
    place = (2 * f + core) % n_fsdp

    def to_home(pieces):
        full = jnp.zeros((n_fsdp,) + pieces.shape[1:], BF)
        for r in range(n_fsdp):
            piece = lax.dynamic_index_in_dim(pieces, f ^ r, 0, keepdims=True)
            got = lax.ppermute(piece, ("seq", "fsdp"), home_pairs(r, False))
            full = lax.dynamic_update_slice(full, got, (place ^ r, 0, 0))
        return full.reshape(-1, pieces.shape[2])

    def from_home(full):
        full = full.reshape(n_fsdp, -1, full.shape[1])
        pieces = jnp.zeros((2 * parts,) + full.shape[1:], BF)
        for r in range(n_fsdp):
            piece = lax.dynamic_index_in_dim(full, place ^ r, 0, keepdims=True)
            got = lax.ppermute(piece, ("seq", "fsdp"), home_pairs(r, True))
            pieces = lax.dynamic_update_slice(pieces, got, (f ^ r, 0, 0))
        return pieces

    inputs = tokens[0].astype(F32)
    gathered = gather_seq(tokens[0])
    blocks = jnp.array([2 * d + b for b in range(2) for d in range(columns)], jnp.int32)
    positions = ((s ^ blocks)[:, None] * tok + jnp.arange(tok, dtype=jnp.int32)[None, :]).reshape(-1)
    doc, places = documents(lengths[0], positions)
    middle = HEAD_DIM // 2
    frequency = 1.0 / ROPE_THETA ** (jnp.arange(middle, dtype=F32) * 2.0 / HEAD_DIM)
    angles = places.astype(F32)[:, None] * frequency[None, :]
    cosine = jnp.cos(angles)[:, None, :]
    sine = jnp.sin(angles)[:, None, :]
    allowed = (doc[:, None] == doc[None, :]) & (positions[None, :] <= positions[:, None])
    split = (group, heads, HEAD_DIM)

    gathered_f = gathered.astype(F32)
    attn_normed = gathered_f * norm_factor(gathered_f)
    attn_low = (attn_normed * attn_gain).astype(BF)
    qkv_raw = mm(attn_low, qkv, NN)
    query_raw = qkv_raw[:, :head_width]
    key_raw = qkv_raw[:, head_width : 2 * head_width]
    value_low = qkv_raw[:, 2 * head_width :].astype(BF)
    squares = jnp.stack(
        [jnp.sum(query_raw * query_raw, axis=1), jnp.sum(key_raw * key_raw, axis=1)]
    ).reshape(2, 2, columns, tok)
    factors = lax.rsqrt(sum_rows_seq(squares) / width + NORM_EPSILON).reshape(2, group, 1)
    query_factor = factors[0]
    key_factor = factors[1]
    query_normed = query_raw * query_factor
    key_normed = key_raw * key_factor
    head_query = rotate((query_normed * query_gain).reshape(split), cosine, sine).astype(BF)
    head_key = rotate((key_normed * key_gain).reshape(split), cosine, sine).astype(BF)
    head_value = value_low.reshape(split)
    scaling = HEAD_DIM ** (-0.5)

    def scores():
        raw = jnp.einsum("bhd,thd->hbt", head_query, head_key, preferred_element_type=F32)
        return jnp.where(allowed[None], raw * scaling, MASKED)

    logits = scores()
    highest = jnp.max(logits, axis=-1, keepdims=True)
    expon = jnp.exp(logits - highest)
    row_total = jnp.sum(expon, axis=-1, keepdims=True)
    log_total = highest + jnp.log(row_total)
    attended = jnp.einsum(
        "hbt,thd->bhd", (expon / row_total).astype(BF), head_value, preferred_element_type=F32
    )
    mixed = attended.reshape(group, head_width).astype(BF)
    half = group // 2
    far_part = mm(mixed[half:], out_w, NN).astype(BF)
    near_part = mm(mixed[:half], out_w, NN)
    residual = inputs + scatter_seq(near_part, far_part)
    ffn_factor = norm_factor(residual)
    ffn_normed = residual * ffn_factor
    ffn_low = (ffn_normed * ffn_gain).astype(BF)
    router_logits = mm(ffn_low, router_t, NT)
    expon_r = jnp.exp(router_logits - jnp.max(router_logits, axis=-1, keepdims=True))
    probs = expon_r / jnp.sum(expon_r, axis=-1, keepdims=True)

    grad_out = cotangent[0].astype(F32)
    cot_x = jnp.stack([cotangent[0]] + [over_fsdp(cotangent[0], d) for d in range(1, n_fsdp)])
    rows_g = both_cores(dispatch(cot_x))
    ffn_x = jnp.stack([ffn_low] + [over_fsdp(ffn_low, d) for d in range(1, n_fsdp)])
    probs_low = probs.astype(BF)
    probs_x = jnp.stack([probs_low] + [over_fsdp(probs_low, d) for d in range(1, n_fsdp)])
    probs_col = jnp.einsum("gte,ed->dgt", probs_x, select, preferred_element_type=F32)
    weighted = (onehot.astype(F32) * probs_col[:, :, None, :]).astype(BF)
    slot_probs = jnp.sum(weighted.astype(F32), axis=3)
    slot_got = [slot_probs[0]] + [over_seq(slot_probs[d], 2 * d) for d in range(1, columns)]
    slot_own = jnp.stack(slot_got)
    row_probs = jnp.stack([slot_own, over_seq(slot_own, 1)]).reshape(-1, 1)
    rows_x = both_cores(dispatch(ffn_x))
    gate_w = to_home(gate_pieces)
    up_w = to_home(up_pieces)
    down_w = to_home(down_pieces)
    gate_value = mm(rows_x, gate_w, NN)
    up_value = mm(rows_x, up_w, NN)
    gate_sigmoid = jax.nn.sigmoid(gate_value)
    hidden = gate_value * gate_sigmoid * up_value
    hidden_low = hidden.astype(BF)
    grad_hidden = mm(rows_g, down_w, NT)
    route_grad = jnp.sum(grad_hidden * hidden_low.astype(F32), axis=1)
    grad_gate = (
        grad_hidden * up_value * gate_sigmoid * (1.0 + gate_value * (1.0 - gate_sigmoid))
    )
    grad_up = grad_hidden * gate_value * gate_sigmoid
    grad_gate_low = grad_gate.astype(BF)
    grad_up_low = grad_up.astype(BF)
    rows_half = rows_x.shape[0] // 2
    piece_shape = (columns, n_fsdp, capacity, width)

    def give_back(near, far):
        total = (near + over_seq(far.astype(BF), 1).astype(F32)).astype(BF).reshape(piece_shape)
        got = [total[0]] + [over_seq(total[d], 2 * d) for d in range(1, columns)]
        joined = jnp.stack(got, axis=1).reshape(n_fsdp, columns * capacity, width)
        matrix = weighted.transpose(1, 3, 0, 2).reshape(n_fsdp, tok, columns * capacity)
        part = jnp.einsum("gtr,grx->gtx", matrix, joined, preferred_element_type=F32)
        low = part.astype(BF)
        result = part[0]
        for d in range(1, n_fsdp):
            result = result + over_fsdp(low[d], d).astype(F32)
        return result

    def entry(a, b):
        return mm(grad_gate_low[a:b], gate_w, NT) + mm(grad_up_low[a:b], up_w, NT)

    far_entry = entry(rows_half, 2 * rows_half)
    near_entry = entry(0, rows_half)
    grad_ffn = give_back(near_entry, far_entry)
    far_out = mm(hidden_low[rows_half:], down_w, NN)
    near_out = mm(hidden_low[:rows_half], down_w, NN)
    outputs = residual + give_back(near_out, far_out)

    route_grad = route_grad.reshape((2,) + piece_shape[:3])
    route_own = route_grad[0] + over_seq(route_grad[1], 1)
    route_back = jnp.stack(
        [route_own[0]] + [over_seq(route_own[d], 2 * d) for d in range(1, columns)]
    )
    grad_col = jnp.sum(onehot.astype(F32) * route_back[:, :, :, None], axis=2)
    grad_probs_x = jnp.sum(
        grad_col[:, :, :, None] * select.T.astype(F32)[:, None, None, :], axis=0
    )
    grad_probs = grad_probs_x[0]
    for d in range(1, n_fsdp):
        grad_probs = grad_probs + over_fsdp(grad_probs_x[d], d)
    grad_logits = (
        probs * (grad_probs - jnp.sum(probs * grad_probs, axis=1, keepdims=True))
    ).astype(BF)
    router_grad = mm(grad_logits, ffn_low, TN)
    grad_ffn = grad_ffn + mm(grad_logits, router_t, NN)
    ffn_gain_grad = jnp.sum(grad_ffn * ffn_normed, axis=0, keepdims=True)
    grad_resid = grad_out + norm_back(grad_ffn, ffn_gain, ffn_normed, ffn_factor)
    grad_attn = grad_resid.astype(BF)

    grad_gate_p = (grad_gate * row_probs).astype(BF)
    grad_up_p = (grad_up * row_probs).astype(BF)
    hidden_p = (hidden * row_probs).astype(BF)
    gate_grad = from_home(mm(rows_x, grad_gate_p, TN).astype(BF))
    up_grad = from_home(mm(rows_x, grad_up_p, TN).astype(BF))
    down_grad = from_home(mm(hidden_p, rows_g, TN).astype(BF))

    def unsplit(pieces):
        return (
            pieces.reshape(2, parts, shard, n_fsdp, ff_piece).transpose(0, 2, 3, 1, 4)
            .reshape(2, shard, ff).astype(F32)
        )

    grad_all = gather_seq(grad_attn)
    out_grad = mm(mixed, grad_all, TN)
    grad_heads = mm(grad_all, out_w, NT).astype(BF).reshape(split)
    weights_soft = jnp.exp(scores() - log_total)
    grad_soft = jnp.einsum("bhd,thd->hbt", grad_heads, head_value, preferred_element_type=F32)
    inner = jnp.sum(weights_soft * grad_soft, axis=-1, keepdims=True)
    grad_raw = (weights_soft * (grad_soft - inner) * scaling).astype(BF)
    grad_query = jnp.einsum("hbt,thd->bhd", grad_raw, head_key, preferred_element_type=F32)
    grad_key = jnp.einsum("hbt,bhd->thd", grad_raw, head_query, preferred_element_type=F32)
    grad_value = jnp.einsum(
        "hbt,bhd->thd", weights_soft.astype(BF), grad_heads, preferred_element_type=F32
    )
    grad_value_low = grad_value.reshape(group, head_width).astype(BF)
    grad_query_rot = rotate(grad_query, cosine, -sine).reshape(group, head_width)
    grad_key_rot = rotate(grad_key, cosine, -sine).reshape(group, head_width)
    query_gain_grad = jnp.sum(grad_query_rot * query_normed, axis=0)
    key_gain_grad = jnp.sum(grad_key_rot * key_normed, axis=0)
    grad_query_n = grad_query_rot * query_gain
    grad_key_n = grad_key_rot * key_gain
    inners = jnp.stack(
        [jnp.sum(grad_query_n * query_normed, axis=1), jnp.sum(grad_key_n * key_normed, axis=1)]
    ).reshape(2, 2, columns, tok)
    inners = (sum_rows_seq(inners) / width).reshape(2, group, 1)
    grad_query_low = (query_factor * (grad_query_n - query_normed * inners[0])).astype(BF)
    grad_key_low = (key_factor * (grad_key_n - key_normed * inners[1])).astype(BF)
    grad_qkv = jnp.concatenate([grad_query_low, grad_key_low, grad_value_low], axis=1)
    far_in = mm(grad_qkv[half:], qkv, NT)
    near_in = mm(grad_qkv[:half], qkv, NT)
    qkv_grad = mm(attn_low, grad_qkv, TN)
    attn_gain_grad = jnp.sum(far_in * attn_normed[half:], axis=0, keepdims=True) + jnp.sum(
        near_in * attn_normed[:half], axis=0, keepdims=True
    )
    grad_in = scatter_seq(near_in, far_in.astype(BF))
    own_factor = norm_factor(inputs)
    tokens_grad = grad_resid + norm_back(grad_in, attn_gain, inputs * own_factor, own_factor)

    def scatter_fsdp(full, axis):
        low = full.astype(BF)
        result = lax.dynamic_slice_in_dim(full, f * shard, shard, axis)
        for d in range(1, n_fsdp):
            piece = lax.dynamic_slice_in_dim(low, (f ^ d) * shard, shard, axis)
            result = result + over_fsdp(piece, d).astype(F32)
        return result

    qkv_own = scatter_fsdp(qkv_grad, 0)
    out_own = scatter_fsdp(out_grad, 1)
    everyone = (("seq", n_seq), ("fsdp", n_fsdp))
    mid_sum = sum_all(jnp.concatenate([ffn_gain_grad, router_grad], axis=0), everyone)
    attn_sum = sum_all(attn_gain_grad, everyone)
    head_sum = sum_all(
        jnp.stack([query_gain_grad, key_gain_grad]), (("fsdp", n_fsdp),)
    )
    mine = width // (n_seq * n_fsdp)
    at = (s * n_fsdp + f) * mine
    mid_own = lax.dynamic_slice_in_dim(mid_sum, at, mine, 1)
    attn_own = lax.dynamic_slice_in_dim(attn_sum, at, mine, 1)
    head_own = lax.dynamic_slice_in_dim(head_sum, f * mine, mine, 1)
    return (
        outputs.astype(BF)[None],
        tokens_grad[None],
        attn_own[0],
        qkv_own[:, :head_width],
        qkv_own[:, head_width : 2 * head_width],
        qkv_own[:, 2 * head_width :],
        out_own,
        head_own[0],
        head_own[1],
        mid_own[0],
        mid_own[1:].T,
        unsplit(gate_grad),
        unsplit(up_grad),
        down_grad.reshape(2, parts * ff_piece, width).astype(F32),
    )


def solution(mesh):
    in_specs = (
        P("fsdp", "seq", None), P("fsdp", "seq", None), P("fsdp", None), P("fsdp", "seq"),
        P("fsdp", "seq", None), P("fsdp"), P("fsdp", "seq"), P("fsdp", "seq"), P("fsdp", "seq"),
        P("seq", "fsdp"), P("fsdp"), P("fsdp"), P("fsdp"), P("fsdp", None),
        P("seq", "fsdp", None), P("seq", "fsdp", None), P("seq", "fsdp", None),
    )
    out_specs = (
        P("fsdp", "seq", None), P("fsdp", "seq", None), P(("seq", "fsdp")), P("fsdp", "seq"),
        P("fsdp", "seq"), P("fsdp", "seq"), P("seq", "fsdp"), P(("seq", "fsdp")),
        P(("seq", "fsdp")), P(("seq", "fsdp")), P(("seq", "fsdp"), None),
        P("seq", "fsdp", None), P("seq", "fsdp", None), P("seq", "fsdp", None),
    )
    return jax.shard_map(body, mesh=mesh, in_specs=in_specs, out_specs=out_specs, check_vma=False)
```
